512 devices in a mesh: row: 32 (over z, x_lo), rep: 16 (over x_hi, y, core).
Axes of the slice: x: 4 (x_hi: 2, x_lo: 2; x = x_hi * 2 + x_lo), y: 4, z: 16, core: 2. Of those that a mesh axis runs over, the one named last changes fastest.
Arguments:
- features: bfloat16 [131072, 256], P(('row', 'rep')), may hold values from -6 to 6
- dense_blocks: bfloat16 [131072, 2, 4096], P('row', None, 'rep'), may hold values from -0.0625 to 0.0625
- thick_neighbour_labels: int32 [32, 2], P('row'), may hold values from 0 to 31, as said below
- tile_source: int32 [32, 16, 64], P('row', 'rep'), may hold values from 0 to 63, as said below
- tile_dest: int32 [32, 16, 64], P('row', 'rep'), may hold values from 0 to 31
- entry_rows: int32 [32, 16, 64, 512], P('row', 'rep'), may hold values from 0 to 127, as said below
- entry_cols: int32 [32, 16, 64, 512], P('row', 'rep'), may hold values from 0 to 127
- edge_strength_list: bfloat16 [32, 16, 64, 512], P('row', 'rep'), may hold values from -0.75 to 0.75
- entry_count: int32 [32, 16, 64], P('row', 'rep'), may hold values from 1 to 512
- weight: bfloat16 [256, 256], replicated, may hold values from -0.375 to 0.375
- out_bias: float32 [256], replicated, may hold values from -3 to 3
Outputs:
- activated: bfloat16 [131072, 256], P(('row', 'rep'))
The draws below stay inside these ranges and needn't reach their ends.
Inputs may be any that keep to these rules, and one draw needn't show every extreme that they name: `thick_neighbour_labels`: each row block's dense source blocks are distinct and lie within cyclic distance 3 of its own block id. Within one device's list, entries with the same source row block (tile_source // 2) name the same tile. The (entry_rows, entry_cols) pairs of one sparse tile's entries are distinct.
All inputs are finite; a program needn't handle non-finite values.
Results may differ from the reference program's by a relative error of at most 0.0047.
Values may be sent and summed in bfloat16 or wider, within the bound.
A program may use at most 64 MiB of HBM per device.

```python
import jax
import jax.numpy as jnp
from jax import lax

FEAT = 256
TILE = 128
TILES_DEV = 2
REACH = 3
DENSE_BLK = 2
LISTED_PER_CHIP = 64
ENTRIES = 512
BLOCK_ROWS = 4096
NODES = 131072
N_ROW = 32
N_REP = 16


def cell_pattern(key):
    cell_total = TILE * TILE
    base_key = jax.random.fold_in(key, 11)
    key_start, key_stride = jax.random.split(base_key)
    cell_shape = (N_ROW, N_REP, LISTED_PER_CHIP, 1)
    starts = jax.random.randint(key_start, cell_shape, 0, cell_total)
    stride_lengths = 2 * jax.random.randint(key_stride, cell_shape, 0, cell_total // 2) + 1
    entry_index = jnp.arange(ENTRIES, dtype=jnp.int32)
    return ((starts + stride_lengths * entry_index) % cell_total).astype(jnp.int32)


def draw_entry_rows(key, part):
    return (cell_pattern(key) // TILE).astype(jnp.int32)


def draw_entry_cols(key, part):
    return (cell_pattern(key) % TILE).astype(jnp.int32)


def draw_entry_count(key, part):
    counts = jax.random.randint(key, (N_ROW, N_REP, LISTED_PER_CHIP), 1, ENTRIES + 1)
    slot_index = jnp.arange(LISTED_PER_CHIP, dtype=jnp.int32)
    return jnp.where(slot_index[None, None, :] == 0, ENTRIES, counts).astype(jnp.int32)


def pick_offsets(row_random_key):
    return jax.random.permutation(row_random_key, 2 * REACH + 1)[:DENSE_BLK].astype(jnp.int32)


def draw_thick_neighbour_labels(key, part):
    row_keys = jax.random.split(key, N_ROW)
    offsets = jax.vmap(pick_offsets)(row_keys)
    own_block = jnp.arange(N_ROW, dtype=jnp.int32)[:, None]
    return ((own_block + offsets - REACH + N_ROW) % N_ROW).astype(jnp.int32)


def draw_tile_source(key, part):
    key_one, key_two, tile_key_split = jax.random.split(key, 3)
    list_shape = (N_ROW, N_REP, LISTED_PER_CHIP)
    nearer = jnp.minimum(jax.random.randint(key_one, list_shape, 0, N_ROW), jax.random.randint(key_two, list_shape, 0, N_ROW))
    own_block = jnp.arange(N_ROW, dtype=jnp.int32)[:, None, None]
    source_block = ((own_block + nearer) % N_ROW).astype(jnp.int32)
    tile_table = jax.random.randint(tile_key_split, (N_ROW, N_REP, N_ROW), 0, TILES_DEV)
    picked = jnp.take_along_axis(tile_table, source_block, axis=2)
    return (source_block * TILES_DEV + picked).astype(jnp.int32)


def place_ends(entries, rng, low, largest):
    shape = entries.shape
    spot = [jax.random.randint(jax.random.fold_in(rng, axis), (), 0, shape[axis]) for axis in range(len(shape))]
    entries = entries.at[tuple(spot)].set(low)
    longest = shape.index(max(shape))
    spot[longest] = (spot[longest] + 1) % shape[longest]
    return entries.at[tuple(spot)].set(largest)


def level_of(stream_key, shape, cuts, least, top_value):
    def one(position, shards_of):
        heights = jax.random.uniform(jax.random.fold_in(jax.random.fold_in(stream_key, 6), position), (shards_of,), jnp.float32, least / len(cuts), top_value / len(cuts))
        return jnp.repeat(jnp.exp(heights), shape[position] // shards_of).reshape((-1,) + (1,) * (len(shape) - position - 1))

    level = one(*cuts[0])
    for cut in cuts[1:]:
        level = level * one(*cut)
    return level


def gaussian(rng, shape, deviation, limit, pieces=(), kind=jnp.bfloat16):
    level = level_of(rng, shape, pieces, -0.22, 0.18) if pieces else 1.0
    drawn = jax.random.normal(rng, shape, jnp.float32) * deviation * level
    return jnp.minimum(jnp.maximum(drawn, -limit), limit).astype(kind)


def setup_inputs(seed: int = 0) -> dict:
    keys = jax.random.split(jax.random.key(seed), 12)
    features = gaussian(keys[0], (NODES, FEAT), 1.0, 6.0, ((0, 512),))
    dense_blocks = gaussian(keys[1], (NODES, DENSE_BLK, BLOCK_ROWS), (DENSE_BLK * BLOCK_ROWS) ** -0.5, 0.0625, ((0, 32), (2, 16)))
    thick_neighbour_labels = draw_thick_neighbour_labels(jax.random.fold_in(keys[11], 71), 0)
    tile_source = draw_tile_source(jax.random.fold_in(keys[11], 71), 0)
    tile_dest = place_ends(jax.random.randint(keys[4], (N_ROW, N_REP, LISTED_PER_CHIP), 0, TILES_DEV * N_REP), jax.random.fold_in(keys[4], 1), 0, (TILES_DEV * N_REP) - 1).astype(jnp.int32)
    entry_rows = draw_entry_rows(jax.random.fold_in(keys[11], 71), 0)
    entry_cols = draw_entry_cols(jax.random.fold_in(keys[11], 71), 0)
    edge_strength_list = gaussian(keys[7], (N_ROW, N_REP, LISTED_PER_CHIP, ENTRIES), 0.125, 0.75, ((0, 32), (1, 16)))
    entry_count = draw_entry_count(jax.random.fold_in(keys[11], 71), 0)
    weight = gaussian(keys[9], (FEAT, FEAT), FEAT ** -0.5, 0.375)
    out_bias = gaussian(keys[10], (FEAT,), 0.5, 3.0, (), jnp.float32)
    return dict(features=features, dense_blocks=dense_blocks, thick_neighbour_labels=thick_neighbour_labels, tile_source=tile_source, tile_dest=tile_dest, entry_rows=entry_rows, entry_cols=entry_cols, edge_strength_list=edge_strength_list, entry_count=entry_count, weight=weight, out_bias=out_bias)


def reference(features, dense_blocks, thick_neighbour_labels, tile_source, tile_dest, entry_rows, entry_cols, edge_strength_list, entry_count, weight, out_bias):
    feat_wide = features.astype(jnp.float32)
    entry_index = jnp.arange(ENTRIES, dtype=jnp.int32)
    rep_index = jnp.arange(N_REP, dtype=jnp.int32)

    def one_block(block_index):
        start_row = (block_index * BLOCK_ROWS).astype(jnp.int32)
        dense_rows = lax.dynamic_slice_in_dim(dense_blocks, start_row, BLOCK_ROWS, 0).astype(jnp.float32)
        running = jnp.zeros((BLOCK_ROWS, FEAT), jnp.float32)
        for slot_index in range(DENSE_BLK):
            first_node = (thick_neighbour_labels[block_index, slot_index] * BLOCK_ROWS).astype(jnp.int32)
            source = lax.dynamic_slice_in_dim(feat_wide, first_node, BLOCK_ROWS, 0)
            running = running + jnp.dot(dense_rows[:, slot_index, :], source, precision=lax.Precision.HIGHEST)
        listed = tile_source[block_index]
        source_block = listed // TILES_DEV
        source_tile_matrix = listed % TILES_DEV
        patch_offset_first = source_block * BLOCK_ROWS + rep_index[:, None] * (TILES_DEV * TILE) + source_tile_matrix * TILE
        source_nodes = (patch_offset_first[:, :, None] + entry_cols[block_index]).astype(jnp.int32)
        dest_rows = (tile_dest[block_index][:, :, None] * TILE + entry_rows[block_index]).astype(jnp.int32)
        active = entry_index[None, None, :] < entry_count[block_index][:, :, None]
        weights_live = jnp.where(active, edge_strength_list[block_index].astype(jnp.float32), jnp.float32(0.0))
        picked = feat_wide[source_nodes.reshape(-1)] * weights_live.reshape(-1, 1)
        running = running + jax.ops.segment_sum(picked, dest_rows.reshape(-1), num_segments=BLOCK_ROWS)
        return running

    block_sums = lax.map(one_block, jnp.arange(N_ROW, dtype=jnp.int32))
    hidden = block_sums.reshape(NODES, FEAT).astype(jnp.bfloat16)
    projected = jnp.dot(hidden, weight, preferred_element_type=jnp.float32) + out_bias
    return jnp.maximum(projected, 0.0).astype(jnp.bfloat16)
```

```python
import functools

import jax
import jax.numpy as jnp
from jax import lax
from jax.experimental import pallas as pl
from jax.experimental.pallas import tpu as pltpu
from jax.sharding import PartitionSpec as P

FEAT = 256
TILE = 128
NEAR = 2
MESH = pl.DeviceIdType.MESH
HALVES = ((1, 3), (3, 1))


def gather_kernel(
    depth,
    labels,
    counts,
    feat,
    rows_ref,
    cols_ref,
    strength,
    dense_hbm,
    got_out,
    acc_out,
    mats_out,
    near,
    far,
    panels,
    dense_v,
    acc_v,
    mats_v,
    send_sem,
    recv_sem,
    local_sem,
):
    me = lax.axis_index("row")
    z = me // 2
    side = me % 2
    mate = {"row": z * 2 + 1 - side}
    ring = (
        {"row": lax.rem(z + 1, depth) * 2 + side},
        {"row": lax.rem(z + depth - 1, depth) * 2 + side},
    )
    step_sign = (1, -1)
    half = depth // 2

    barrier = pltpu.get_barrier_semaphore()
    for peer in (mate,) + ring:
        pl.semaphore_signal(barrier, inc=1, device_id=peer, device_id_type=MESH)

    dense_in = pltpu.make_async_copy(dense_hbm, dense_v, local_sem.at[0])
    dense_in.start()
    near[NEAR * 2] = feat[...]
    pl.semaphore_wait(barrier, 3)

    def spot(offset, column, tile):
        rows = pl.ds(tile * TILE, TILE)
        offset = depth - half if offset == -half else offset
        if -NEAR <= offset <= NEAR:
            return near.at[(offset + NEAR) * 2 + column, rows]
        place = offset + half - 1 if offset < 0 else offset + half - 2 - 2 * NEAR
        return far.at[place * 2 + column, rows]

    pieces = ((0, 0), (0, 1), (1, 1))
    last = ((half, half - 1), (half - 1, half), (half, half - 1))
    started = []

    def ring_copy(piece, way, step):
        column, tile = pieces[piece]
        sign = step_sign[way]
        here = -sign * (step - 1)
        index = (piece * 2 + way) * half + step - 1
        source = feat.at[pl.ds(tile * TILE, TILE)] if here == 0 and column == 0 else spot(here, column, tile)
        return pltpu.make_async_remote_copy(
            src_ref=source,
            dst_ref=spot(-sign * step, column, tile),
            send_sem=send_sem.at[index],
            recv_sem=recv_sem.at[index],
            device_id=ring[way],
            device_id_type=MESH,
        )

    def mate_copy(offset, tile):
        offset = depth - half if offset == -half else offset
        index = 6 * half + (depth if tile else offset + half - 1)
        source = feat.at[pl.ds(tile * TILE, TILE)] if offset == 0 else spot(offset, 0, tile)
        return pltpu.make_async_remote_copy(
            src_ref=source,
            dst_ref=spot(offset, 1, tile),
            send_sem=send_sem.at[index],
            recv_sem=recv_sem.at[index],
            device_id=mate,
            device_id_type=MESH,
        )

    def begin(copy):
        copy.start()
        started.append(copy)

    positions = lax.broadcasted_iota(jnp.int32, (TILE, rows_ref.shape[1]), 0)
    lanes = lax.broadcasted_iota(jnp.int32, (1, rows_ref.shape[1]), 1)

    def build_mats(first, stop):
        def body(i, carry):
            live = jnp.where(lanes < counts[0, i], strength[pl.ds(i, 1), :], 0.0)
            at_row = jnp.where(positions == rows_ref[pl.ds(i, 1), :], 1.0, 0.0).astype(jnp.bfloat16)
            at_col = jnp.where(positions == cols_ref[pl.ds(i, 1), :], live, 0.0).astype(jnp.bfloat16)
            mats_v[i] = lax.dot_general(
                at_row, at_col, (((1,), (1,)), ((), ())), preferred_element_type=jnp.float32
            ).astype(jnp.bfloat16)
            return carry

        lax.fori_loop(first, stop, body, 0)

    chunk = 256
    chunks = acc_v.shape[0] // chunk

    def dense_part(first, stop):
        def body(i, carry):
            rows = pl.ds(pl.multiple_of(i * chunk, chunk), chunk)
            acc_v[rows, :] = jnp.dot(
                dense_v[rows, :], panels[...], preferred_element_type=jnp.float32
            )
            return carry

        lax.fori_loop(first, stop, body, 0)

    def fetch_panels():
        for slot in range(2):
            label = labels[0, slot]
            offset = jnp.minimum(lax.rem(label // 2 - z + NEAR + depth, depth), 2 * NEAR)
            column = lax.rem(label + side, 2)
            panels[pl.ds(slot * FEAT, FEAT), :] = near[offset * 2 + column]

    begin(mate_copy(0, 1))
    for piece in (0, 1):
        for way in (0, 1):
            begin(ring_copy(piece, way, 1))
    begin(mate_copy(0, 0))
    mate_copy(0, 1).wait_recv()
    for way in (0, 1):
        begin(ring_copy(2, way, 1))

    tiles = mats_v.shape[0]
    early = 3 * (NEAR + 1)
    late = 3 * (half - NEAR - 1)
    slot = 0
    for step in range(1, half + 1):
        for piece in range(3):
            if slot < early:
                build_mats(slot * tiles // early, (slot + 1) * tiles // early)
            else:
                if slot == early:
                    mate_copy(0, 0).wait_recv()
                    for near_step in range(1, NEAR + 1):
                        for sign in step_sign:
                            mate_copy(-sign * near_step, 0).wait_recv()
                    fetch_panels()
                    dense_in.wait()
                dense_part((slot - early) * chunks // late, (slot - early + 1) * chunks // late)
            for way in (0, 1):
                if step <= last[piece][way]:
                    ring_copy(piece, way, step).wait_recv()
                    if step < last[piece][way]:
                        begin(ring_copy(piece, way, step + 1))
                    if piece == 0:
                        begin(mate_copy(-step_sign[way] * step, 0))
            slot += 1
    acc_copy = pltpu.make_async_copy(acc_v, acc_out, local_sem.at[1])
    acc_copy.start()
    mats_copy = pltpu.make_async_copy(mats_v, mats_out, local_sem.at[2])
    mats_copy.start()
    near_copy = pltpu.make_async_copy(near, got_out.at[pl.ds(0, near.shape[0])], local_sem.at[3])
    near_copy.start()
    for offset in range(NEAR + 1, half + 1):
        mate_copy(offset, 0).wait_recv()
        if offset < half:
            mate_copy(-offset, 0).wait_recv()
    far_copy = pltpu.make_async_copy(
        far, got_out.at[pl.ds(near.shape[0], far.shape[0])], local_sem.at[4]
    )
    far_copy.start()
    for copy in started:
        copy.wait_send()
    for copy in (acc_copy, mats_copy, near_copy, far_copy):
        copy.wait()


def gather_and_prepare(features, dense_blocks, labels, counts, rows, cols, strength):
    depth = lax.axis_size("row") // 2
    block_rows = dense_blocks.shape[0]
    tiles = rows.shape[0]
    near = 2 * (2 * NEAR + 1)
    far = 2 * depth - near
    sems = 3 * depth + depth + 1
    vmem = pl.BlockSpec(memory_space=pltpu.VMEM)
    smem = pl.BlockSpec(memory_space=pltpu.SMEM)
    anywhere = pl.BlockSpec(memory_space=pl.ANY)
    return pl.pallas_call(
        functools.partial(gather_kernel, depth),
        out_shape=(
            jax.ShapeDtypeStruct((near + far, FEAT, FEAT), jnp.bfloat16),
            jax.ShapeDtypeStruct((block_rows, FEAT), jnp.float32),
            jax.ShapeDtypeStruct((tiles, TILE, TILE), jnp.bfloat16),
        ),
        in_specs=[smem, smem, vmem, vmem, vmem, vmem, anywhere],
        out_specs=(anywhere, anywhere, anywhere),
        scratch_shapes=[
            pltpu.VMEM((near, FEAT, FEAT), jnp.bfloat16),
            pltpu.VMEM((far, FEAT, FEAT), jnp.bfloat16),
            pltpu.VMEM((2 * FEAT, FEAT), jnp.bfloat16),
            pltpu.VMEM(dense_blocks.shape, jnp.bfloat16),
            pltpu.VMEM((block_rows, FEAT), jnp.float32),
            pltpu.VMEM((tiles, TILE, TILE), jnp.bfloat16),
            pltpu.SemaphoreType.DMA((sems,)),
            pltpu.SemaphoreType.DMA((sems,)),
            pltpu.SemaphoreType.DMA((5,)),
        ],
        compiler_params=pltpu.CompilerParams(collective_id=0, has_side_effects=True),
        name="gather_and_prepare",
    )(labels, counts, features, rows, cols, strength, dense_blocks)


def place_kernel(source, dest, got, mats, acc_hbm, out, acc, sem):
    copy = pltpu.make_async_copy(acc_hbm, acc, sem)
    copy.start()
    copy.wait()

    def body(i, carry):
        rows = pl.ds(pl.multiple_of(dest[0, i] * TILE, TILE), TILE)
        acc[rows, :] += jnp.dot(
            mats[i], got[source[0, i]], preferred_element_type=jnp.float32
        )
        return carry

    lax.fori_loop(0, mats.shape[0], body, 0)
    out[...] = acc[...].astype(jnp.bfloat16)


def place_tiles(source, dest, got, mats, acc):
    vmem = pl.BlockSpec(memory_space=pltpu.VMEM)
    smem = pl.BlockSpec(memory_space=pltpu.SMEM)
    return pl.pallas_call(
        place_kernel,
        out_shape=jax.ShapeDtypeStruct(acc.shape, jnp.bfloat16),
        in_specs=[smem, smem, vmem, vmem, pl.BlockSpec(memory_space=pl.ANY)],
        out_specs=vmem,
        scratch_shapes=[pltpu.VMEM(acc.shape, jnp.float32), pltpu.SemaphoreType.DMA],
        name="place_tiles",
    )(source, dest, got, mats, acc)


def scatter_kernel(
    part, weight, bias, out, from_core, sum_core, from_one, sum_one, from_two, sum_two, from_x, send_sem, recv_sem
):
    me = lax.axis_index("rep")
    core = me % 2
    y = (me // 2) % 4
    x = me // 8

    def rep_of(xx, yy, cc):
        return (xx * 4 + yy) * 2 + cc

    flips = (y, y + 1 - 2 * (y % 2), (y + 2) % 4, 3 - y)
    mate = {"rep": rep_of(x, y, 1 - core)}
    y_peer = {1: {"rep": rep_of(x, flips[1], core)}, 3: {"rep": rep_of(x, flips[3], core)}}
    x_peer = {"rep": rep_of(1 - x, y, core)}
    barrier = pltpu.get_barrier_semaphore()
    for peer in (mate, y_peer[1], y_peer[3], x_peer):
        pl.semaphore_signal(barrier, inc=1, device_id=peer, device_id_type=MESH)
    pl.semaphore_wait(barrier, 4)

    def piece(h, q, t, cc):
        xx = x if q == 0 else 1 - x
        first = rep_of(xx, flips[t], cc) * (2 * TILE) + h * TILE
        return part.at[pl.ds(pl.multiple_of(first, TILE), TILE)]

    def number(h, q, t):
        return (h * 2 + q) * 4 + t

    def remote(source, target, index, peer):
        return pltpu.make_async_remote_copy(
            src_ref=source,
            dst_ref=target,
            send_sem=send_sem.at[index],
            recv_sem=recv_sem.at[index],
            device_id=peer,
            device_id_type=MESH,
        )

    def core_copy(h, q, t):
        n = number(h, q, t)
        return remote(piece(h, q, t, 1 - core), from_core.at[n], n, mate)

    def one_copy(h, q, t):
        way = HALVES[h][0]
        arrives = {1: {1: 0, 2: 3}, 3: {3: 0, 2: 1}}[way][t]
        slot = (h * 2 + q) * 2 + (0 if arrives == 0 else 1)
        return remote(sum_core.at[slot], from_one.at[slot], 16 + slot, y_peer[way])

    def two_copy(h, q):
        slot = h * 2 + q
        return remote(sum_two.at[slot], from_two.at[slot], 24 + slot, y_peer[HALVES[h][1]])

    def x_copy(h):
        return remote(sum_one.at[h], from_x.at[h], 28 + h, x_peer)

    def wide(ref):
        return ref[...].astype(jnp.float32)

    started = []

    def begin(copy):
        copy.start()
        started.append(copy)

    first_order = [(h, q, t) for t in (0, 1) for q in (1, 0) for h in (0, 1)]
    sends_one = [(h, q, 2 if k == 0 else HALVES[h][0]) for (h, q, k) in first_order]
    stays = [(h, q, HALVES[h][1]) for q in (1, 0) for h in (0, 1)]
    ends = [(h, q, 0) for q in (1, 0) for h in (0, 1)]
    for key in sends_one + stays + ends:
        begin(core_copy(*key))
    for h, q, t in sends_one:
        copy = one_copy(h, q, t)
        core_copy(h, q, t).wait_recv()
        way = HALVES[h][0]
        slot = (h * 2 + q) * 2 + (0 if t == way else 1)
        sum_core[slot] = (
            wide(piece(h, q, t, core)) + wide(from_core.at[number(h, q, t)])
        ).astype(jnp.bfloat16)
        begin(copy)
    for h, q, t in stays:
        core_copy(h, q, t).wait_recv()
        one_copy(h, q, 2).wait_recv()
        sum_two[h * 2 + q] = (
            wide(piece(h, q, t, core))
            + wide(from_core.at[number(h, q, t)])
            + wide(from_one.at[(h * 2 + q) * 2 + 1])
        ).astype(jnp.bfloat16)
        begin(two_copy(h, q))

    def total(h, q):
        core_copy(h, q, 0).wait_recv()
        one_copy(h, q, HALVES[h][0]).wait_recv()
        two_copy(h, q).wait_recv()
        return (
            wide(piece(h, q, 0, core))
            + wide(from_core.at[number(h, q, 0)])
            + wide(from_one.at[(h * 2 + q) * 2])
            + wide(from_two.at[h * 2 + q])
        )

    for h in (0, 1):
        sum_one[h] = total(h, 1).astype(jnp.bfloat16)
        begin(x_copy(h))
    for h in (0, 1):
        own = total(h, 0)
        x_copy(h).wait_recv()
        hidden = (own + wide(from_x.at[h])).astype(jnp.bfloat16)
        projected = jnp.dot(hidden, weight[...], preferred_element_type=jnp.float32) + bias[...]
        out[pl.ds(h * TILE, TILE), :] = jnp.maximum(projected, 0.0).astype(jnp.bfloat16)
    for copy in started:
        copy.wait_send()


def scatter_and_project(part, weight, bias):
    vmem = pl.BlockSpec(memory_space=pltpu.VMEM)

    def tiles(n):
        return pltpu.VMEM((n, TILE, FEAT), jnp.bfloat16)

    return pl.pallas_call(
        scatter_kernel,
        out_shape=jax.ShapeDtypeStruct((2 * TILE, FEAT), jnp.bfloat16),
        in_specs=[vmem, vmem, vmem],
        out_specs=vmem,
        scratch_shapes=[
            tiles(16),
            tiles(8),
            tiles(8),
            tiles(2),
            tiles(4),
            tiles(4),
            tiles(2),
            pltpu.SemaphoreType.DMA((30,)),
            pltpu.SemaphoreType.DMA((30,)),
        ],
        compiler_params=pltpu.CompilerParams(collective_id=1, has_side_effects=True),
        name="scatter_and_project",
    )(part, weight, bias)


def shards(
    features,
    dense_blocks,
    thick_neighbour_labels,
    tile_source,
    tile_dest,
    entry_rows,
    entry_cols,
    edge_strength_list,
    entry_count,
    weight,
    out_bias,
):
    depth = lax.axis_size("row") // 2
    block_rows = dense_blocks.shape[0]
    me = lax.axis_index("row")
    got, acc, mats = gather_and_prepare(
        features,
        dense_blocks.reshape(block_rows, 2 * FEAT),
        thick_neighbour_labels,
        entry_count[0],
        entry_rows[0, 0],
        entry_cols[0, 0],
        edge_strength_list[0, 0].astype(jnp.float32),
    )
    half = depth // 2
    block = tile_source[0] // 2
    offset = (block // 2 - me // 2 + half - 1 + depth) % depth - (half - 1)
    near_place = offset + NEAR
    far_place = 2 * NEAR + 1 + jnp.where(offset < 0, offset + half - 1, offset + half - 2 - 2 * NEAR)
    place = jnp.where(jnp.abs(offset) <= NEAR, near_place, far_place)
    source = (place * 2 + (block + me) % 2) * 2 + tile_source[0] % 2
    part = place_tiles(
        source.astype(jnp.int32),
        tile_dest[0],
        got.reshape(4 * depth, TILE, FEAT),
        mats,
        acc,
    )
    return scatter_and_project(part, weight, out_bias.reshape(1, FEAT))


def solution(mesh):
    return jax.shard_map(
        shards,
        mesh=mesh,
        in_specs=(
            P(("row", "rep"), None),
            P("row", None, "rep"),
            P("row", None),
            P("row", "rep", None),
            P("row", "rep", None),
            P("row", "rep", None, None),
            P("row", "rep", None, None),
            P("row", "rep", None, None),
            P("row", "rep", None),
            P(),
            P(),
        ),
        out_specs=P(("row", "rep"), None),
        check_vma=False,
    )
```

```python
import functools

import jax
import jax.numpy as jnp
from jax import lax
from jax.experimental import pallas as pl
from jax.experimental.pallas import tpu as pltpu
from jax.sharding import PartitionSpec as P

FEAT = 256
TILE = 128
NEAR = 2
BY_MATE = (4, 6)
MESH = pl.DeviceIdType.MESH
HALVES = ((1, 3), (3, 1))


def gather_kernel(
    depth,
    labels,
    counts,
    feat,
    rows_ref,
    cols_ref,
    strength_in,
    dense_v,
    got,
    acc_v,
    mats_v,
    panels,
    mixed,
    strength,
    send_sem,
    recv_sem,
):
    me = lax.axis_index("row")
    z = me // 2
    side = me % 2
    mate = {"row": z * 2 + 1 - side}
    ring = (
        {"row": lax.rem(z + 1, depth) * 2 + side},
        {"row": lax.rem(z + depth - 1, depth) * 2 + side},
    )
    step_sign = (1, -1)
    half = depth // 2

    barrier = pltpu.get_barrier_semaphore()
    for peer in (mate,) + ring:
        pl.semaphore_signal(barrier, inc=1, device_id=peer, device_id_type=MESH)

    got[2 * (half - 1)] = feat[...]
    strength[...] = strength_in[...].astype(jnp.float32)
    pl.semaphore_wait(barrier, 3)

    def spot(offset, column, tile):
        rows = pl.ds(tile * TILE, TILE)
        offset = depth - half if offset == -half else offset
        return got.at[(offset + half - 1) * 2 + column, rows]

    pieces = ((0, 0), (0, 1), (1, 1))
    last = ((half, half - 1), (half - 1, half), (half, half - 1))
    started = []

    def ring_copy(piece, way, step):
        column, tile = pieces[piece]
        sign = step_sign[way]
        here = -sign * (step - 1)
        index = (piece * 2 + way) * half + step - 1
        source = feat.at[pl.ds(tile * TILE, TILE)] if here == 0 and column == 0 else spot(here, column, tile)
        return pltpu.make_async_remote_copy(
            src_ref=source,
            dst_ref=spot(-sign * step, column, tile),
            send_sem=send_sem.at[index],
            recv_sem=recv_sem.at[index],
            device_id=ring[way],
            device_id_type=MESH,
        )

    def mate_copy(offset, tile):
        offset = depth - half if offset == -half else offset
        index = 6 * half + offset + half - 1
        if tile:
            index = 7 * half + depth // 2
            if offset:
                index += 1 + 2 * BY_MATE.index(abs(offset)) + (offset > 0)
        source = feat.at[pl.ds(tile * TILE, TILE)] if offset == 0 else spot(offset, 0, tile)
        return pltpu.make_async_remote_copy(
            src_ref=source,
            dst_ref=spot(offset, 1, tile),
            send_sem=send_sem.at[index],
            recv_sem=recv_sem.at[index],
            device_id=mate,
            device_id_type=MESH,
        )

    def begin(copy):
        copy.start()
        started.append(copy)

    positions = lax.broadcasted_iota(jnp.int32, (TILE, rows_ref.shape[1]), 0)
    lanes = lax.broadcasted_iota(jnp.int32, (1, rows_ref.shape[1]), 1)

    def build_mats(first, stop):
        def body(i, carry):
            live = jnp.where(lanes < counts[0, i], strength[pl.ds(i, 1), :], 0.0)
            at_row = jnp.where(positions == rows_ref[pl.ds(i, 1), :], 1.0, 0.0).astype(jnp.bfloat16)
            at_col = jnp.where(positions == cols_ref[pl.ds(i, 1), :], live, 0.0).astype(jnp.bfloat16)
            mats_v[i] = lax.dot_general(
                at_row, at_col, (((1,), (1,)), ((), ())), preferred_element_type=jnp.float32
            ).astype(jnp.bfloat16)
            return carry

        lax.fori_loop(first, stop, body, 0)

    chunk = 256
    chunks = acc_v.shape[0] // chunk

    def dense_part(first, stop):
        def body(i, carry):
            rows = pl.ds(pl.multiple_of(i * chunk, chunk), chunk)
            both = jnp.dot(
                dense_v[rows].reshape(2 * chunk, FEAT), panels[...], preferred_element_type=jnp.float32
            )
            for lane in range(4):
                mixed[lane] = both[:, lane * TILE : (lane + 1) * TILE]
            for lane in range(2):
                acc_v[rows, pl.ds(lane * TILE, TILE)] = (
                    mixed[lane, pl.ds(0, chunk, stride=2), :] + mixed[lane + 2, pl.ds(1, chunk, stride=2), :]
                )
            return carry

        lax.fori_loop(first, stop, body, 0)

    def fetch_panels():
        for slot in range(2):
            label = labels[0, slot]
            wanted = lax.rem(label // 2 - z + NEAR + depth, depth) * 2 + lax.rem(label + side, 2)
            first = 2 * (half - 1 - NEAR)
            panel = got[first]
            for k in range(1, 2 * (2 * NEAR + 1)):
                panel = jnp.where(wanted == k, got[first + k], panel)
            panels[:, pl.ds(slot * FEAT, FEAT)] = panel

    begin(mate_copy(0, 1))
    for piece in (0, 1):
        for way in (0, 1):
            begin(ring_copy(piece, way, 1))
    begin(mate_copy(0, 0))
    mate_copy(0, 1).wait_recv()
    for way in (0, 1):
        begin(ring_copy(2, way, 1))

    tiles = mats_v.shape[0]
    early = 3 * (NEAR + 1)
    late = 3 * (half - NEAR - 1)
    slot = 0
    for step in range(1, half + 1):
        for piece in range(3):
            if slot < early:
                build_mats(slot * tiles // early, (slot + 1) * tiles // early)
            else:
                if slot == early:
                    mate_copy(0, 0).wait_recv()
                    for near_step in range(1, NEAR + 1):
                        for sign in step_sign:
                            mate_copy(-sign * near_step, 0).wait_recv()
                    fetch_panels()
                dense_part((slot - early) * chunks // late, (slot - early + 1) * chunks // late)
            for way in (0, 1):
                if step <= last[piece][way]:
                    away = -step_sign[way] * step
                    if piece == 2 and step in BY_MATE:
                        mate_copy(away, 1).wait_recv()
                    else:
                        ring_copy(piece, way, step).wait_recv()
                    if step < last[piece][way] and not (piece == 2 and step + 1 in BY_MATE):
                        begin(ring_copy(piece, way, step + 1))
                    if piece == 0 or piece == 1 and step in BY_MATE:
                        begin(mate_copy(away, piece))
            slot += 1
    for offset in range(NEAR + 1, half + 1):
        mate_copy(offset, 0).wait_recv()
        if offset < half:
            mate_copy(-offset, 0).wait_recv()
    for copy in started:
        copy.wait_send()


def gather_and_prepare(features, dense_blocks, labels, counts, rows, cols, strength):
    depth = lax.axis_size("row") // 2
    block_rows = dense_blocks.shape[0]
    tiles = rows.shape[0]
    sems = 3 * depth + depth + 1 + 2 * len(BY_MATE)
    vmem = pl.BlockSpec(memory_space=pltpu.VMEM)
    smem = pl.BlockSpec(memory_space=pltpu.SMEM)
    return pl.pallas_call(
        functools.partial(gather_kernel, depth),
        out_shape=(
            jax.ShapeDtypeStruct((2 * depth, FEAT, FEAT), jnp.bfloat16),
            jax.ShapeDtypeStruct((block_rows, FEAT), jnp.float32),
            jax.ShapeDtypeStruct((tiles, TILE, TILE), jnp.bfloat16),
        ),
        in_specs=[smem, smem, vmem, vmem, vmem, vmem, vmem],
        out_specs=(vmem, vmem, vmem),
        scratch_shapes=[
            pltpu.VMEM((FEAT, 2 * FEAT), jnp.bfloat16),
            pltpu.VMEM((4, 2 * FEAT, TILE), jnp.float32),
            pltpu.VMEM(rows.shape, jnp.float32),
            pltpu.SemaphoreType.DMA((sems,)),
            pltpu.SemaphoreType.DMA((sems,)),
        ],
        compiler_params=pltpu.CompilerParams(collective_id=0, has_side_effects=True, vmem_limit_bytes=20 * 2**20),
        name="gather_and_prepare",
    )(labels, counts, features, rows, cols, strength, dense_blocks)


def place_kernel(depth, source, dest, got, mats, dense, out, acc):
    acc[...] = jnp.zeros_like(acc)
    me = lax.axis_index("row")
    half = depth // 2
    group = 4

    def spot(i):
        listed = source[0, i]
        block = lax.div(listed, 2)
        offset = lax.rem(lax.div(block, 2) - lax.div(me, 2) + half - 1 + depth, depth)
        return (offset * 2 + lax.rem(block + me, 2)) * 2 + lax.rem(listed, 2)

    def body(g, carry):
        terms = [
            jnp.dot(
                mats[g * group + k], got[spot(g * group + k)], preferred_element_type=jnp.float32
            )
            for k in range(group)
        ]
        for k in range(group):
            rows = pl.ds(pl.multiple_of(dest[0, g * group + k] * TILE, TILE), TILE)
            acc[rows, :] += terms[k]
        return carry

    lax.fori_loop(0, mats.shape[0] // group, body, 0)
    out[...] = (acc[...] + dense[...]).astype(jnp.bfloat16)


def place_tiles(source, dest, got, mats, acc):
    vmem = pl.BlockSpec(memory_space=pltpu.VMEM)
    smem = pl.BlockSpec(memory_space=pltpu.SMEM)
    return pl.pallas_call(
        functools.partial(place_kernel, lax.axis_size("row") // 2),
        out_shape=jax.ShapeDtypeStruct(acc.shape, jnp.bfloat16),
        in_specs=[smem, smem, vmem, vmem, vmem],
        out_specs=vmem,
        scratch_shapes=[pltpu.VMEM(acc.shape, jnp.float32)],
        compiler_params=pltpu.CompilerParams(vmem_limit_bytes=20 * 2**20),
        name="place_tiles",
    )(source, dest, got, mats, acc)


def scatter_kernel(
    part, weight, bias, out, from_core, sum_core, from_one, sum_one, from_two, sum_two, from_x, send_sem, recv_sem
):
    me = lax.axis_index("rep")
    core = me % 2
    y = (me // 2) % 4
    x = me // 8

    def rep_of(xx, yy, cc):
        return (xx * 4 + yy) * 2 + cc

    flips = (y, y + 1 - 2 * (y % 2), (y + 2) % 4, 3 - y)
    mate = {"rep": rep_of(x, y, 1 - core)}
    y_peer = {1: {"rep": rep_of(x, flips[1], core)}, 3: {"rep": rep_of(x, flips[3], core)}}
    x_peer = {"rep": rep_of(1 - x, y, core)}
    barrier = pltpu.get_barrier_semaphore()
    for peer in (mate, y_peer[1], y_peer[3], x_peer):
        pl.semaphore_signal(barrier, inc=1, device_id=peer, device_id_type=MESH)
    pl.semaphore_wait(barrier, 4)

    def piece(h, q, t, cc):
        xx = x if q == 0 else 1 - x
        first = rep_of(xx, flips[t], cc) * (2 * TILE) + h * TILE
        return part.at[pl.ds(pl.multiple_of(first, TILE), TILE)]

    def number(h, q, t):
        return (h * 2 + q) * 4 + t

    def remote(source, target, index, peer):
        return pltpu.make_async_remote_copy(
            src_ref=source,
            dst_ref=target,
            send_sem=send_sem.at[index],
            recv_sem=recv_sem.at[index],
            device_id=peer,
            device_id_type=MESH,
        )

    def core_copy(h, q, t):
        n = number(h, q, t)
        return remote(piece(h, q, t, 1 - core), from_core.at[n], n, mate)

    def one_copy(h, q, t):
        way = HALVES[h][0]
        arrives = {1: {1: 0, 2: 3}, 3: {3: 0, 2: 1}}[way][t]
        slot = (h * 2 + q) * 2 + (0 if arrives == 0 else 1)
        return remote(sum_core.at[slot], from_one.at[slot], 16 + slot, y_peer[way])

    def two_copy(h, q):
        slot = h * 2 + q
        return remote(sum_two.at[slot], from_two.at[slot], 24 + slot, y_peer[HALVES[h][1]])

    def x_copy(h):
        return remote(sum_one.at[h], from_x.at[h], 28 + h, x_peer)

    def wide(ref):
        return ref[...].astype(jnp.float32)

    started = []

    def begin(copy):
        copy.start()
        started.append(copy)

    first_order = [(h, q, t) for t in (0, 1) for q in (1, 0) for h in (0, 1)]
    sends_one = [(h, q, 2 if k == 0 else HALVES[h][0]) for (h, q, k) in first_order]
    stays = [(h, q, HALVES[h][1]) for q in (1, 0) for h in (0, 1)]
    ends = [(h, q, 0) for q in (1, 0) for h in (0, 1)]
    for key in sends_one + stays + ends:
        begin(core_copy(*key))
    for h, q, t in sends_one:
        copy = one_copy(h, q, t)
        core_copy(h, q, t).wait_recv()
        way = HALVES[h][0]
        slot = (h * 2 + q) * 2 + (0 if t == way else 1)
        sum_core[slot] = (
            wide(piece(h, q, t, core)) + wide(from_core.at[number(h, q, t)])
        ).astype(jnp.bfloat16)
        begin(copy)
    for h, q, t in stays:
        core_copy(h, q, t).wait_recv()
        one_copy(h, q, 2).wait_recv()
        sum_two[h * 2 + q] = (
            wide(piece(h, q, t, core))
            + wide(from_core.at[number(h, q, t)])
            + wide(from_one.at[(h * 2 + q) * 2 + 1])
        ).astype(jnp.bfloat16)
        begin(two_copy(h, q))

    def total(h, q):
        core_copy(h, q, 0).wait_recv()
        one_copy(h, q, HALVES[h][0]).wait_recv()
        two_copy(h, q).wait_recv()
        return (
            wide(piece(h, q, 0, core))
            + wide(from_core.at[number(h, q, 0)])
            + wide(from_one.at[(h * 2 + q) * 2])
            + wide(from_two.at[h * 2 + q])
        )

    for h in (0, 1):
        sum_one[h] = total(h, 1).astype(jnp.bfloat16)
        begin(x_copy(h))
    for h in (0, 1):
        own = total(h, 0)
        x_copy(h).wait_recv()
        hidden = (own + wide(from_x.at[h])).astype(jnp.bfloat16)
        projected = jnp.dot(hidden, weight[...], preferred_element_type=jnp.float32) + bias[...]
        out[pl.ds(h * TILE, TILE), :] = jnp.maximum(projected, 0.0).astype(jnp.bfloat16)
    for copy in started:
        copy.wait_send()


def scatter_and_project(part, weight, bias):
    vmem = pl.BlockSpec(memory_space=pltpu.VMEM)

    def tiles(n):
        return pltpu.VMEM((n, TILE, FEAT), jnp.bfloat16)

    return pl.pallas_call(
        scatter_kernel,
        out_shape=jax.ShapeDtypeStruct((2 * TILE, FEAT), jnp.bfloat16),
        in_specs=[vmem, vmem, vmem],
        out_specs=vmem,
        scratch_shapes=[
            tiles(16),
            tiles(8),
            tiles(8),
            tiles(2),
            tiles(4),
            tiles(4),
            tiles(2),
            pltpu.SemaphoreType.DMA((30,)),
            pltpu.SemaphoreType.DMA((30,)),
        ],
        compiler_params=pltpu.CompilerParams(collective_id=1, has_side_effects=True, vmem_limit_bytes=10 * 2**20),
        name="scatter_and_project",
    )(part, weight, bias)


def shards(
    features,
    dense_blocks,
    thick_neighbour_labels,
    tile_source,
    tile_dest,
    entry_rows,
    entry_cols,
    edge_strength_list,
    entry_count,
    weight,
    out_bias,
):
    depth = lax.axis_size("row") // 2
    got, acc, mats = gather_and_prepare(
        features,
        dense_blocks,
        thick_neighbour_labels,
        entry_count[0],
        entry_rows[0, 0],
        entry_cols[0, 0],
        edge_strength_list[0, 0],
    )
    part = place_tiles(
        tile_source[0],
        tile_dest[0],
        got.reshape(4 * depth, TILE, FEAT),
        mats,
        acc,
    )
    return scatter_and_project(part, weight, out_bias.reshape(1, FEAT))


def solution(mesh):
    return jax.shard_map(
        shards,
        mesh=mesh,
        in_specs=(
            P(("row", "rep"), None),
            P("row", None, "rep"),
            P("row", None),
            P("row", "rep", None),
            P("row", "rep", None),
            P("row", "rep", None, None),
            P("row", "rep", None, None),
            P("row", "rep", None, None),
            P("row", "rep", None),
            P(),
            P(),
        ),
        out_specs=P(("row", "rep"), None),
        check_vma=False,
    )
```

```python
import functools

import jax
import jax.numpy as jnp
from jax import lax
from jax.experimental import pallas as pl
from jax.experimental.pallas import tpu as pltpu
from jax.sharding import PartitionSpec as P

FEAT = 256
TILE = 128
NEAR = 2
BY_MATE = (4, 6)
MESH = pl.DeviceIdType.MESH
HALVES = ((1, 3), (3, 1))


def gather_kernel(
    depth,
    labels,
    counts,
    feat,
    rows_ref,
    cols_ref,
    strength_in,
    dense_hbm,
    got,
    acc_v,
    mats_v,
    panels,
    mixed,
    strength,
    dense_v,
    send_sem,
    recv_sem,
    local_sem,
):
    me = lax.axis_index("row")
    z = me // 2
    side = me % 2
    mate = {"row": z * 2 + 1 - side}
    ring = (
        {"row": lax.rem(z + 1, depth) * 2 + side},
        {"row": lax.rem(z + depth - 1, depth) * 2 + side},
    )
    step_sign = (1, -1)
    half = depth // 2

    barrier = pltpu.get_barrier_semaphore()
    for peer in (mate,) + ring:
        pl.semaphore_signal(barrier, inc=1, device_id=peer, device_id_type=MESH)

    dense_in = pltpu.make_async_copy(dense_hbm, dense_v, local_sem)
    dense_in.start()
    got[2 * (half - 1)] = feat[...]
    strength[...] = strength_in[...].astype(jnp.float32)
    pl.semaphore_wait(barrier, 3)

    def spot(offset, column, tile):
        rows = pl.ds(tile * TILE, TILE)
        offset = depth - half if offset == -half else offset
        return got.at[(offset + half - 1) * 2 + column, rows]

    pieces = ((0, 0), (0, 1), (1, 1))
    last = ((half, half - 1), (half - 1, half), (half, half - 1))
    started = []

    def ring_copy(piece, way, step):
        column, tile = pieces[piece]
        sign = step_sign[way]
        here = -sign * (step - 1)
        index = (piece * 2 + way) * half + step - 1
        source = feat.at[pl.ds(tile * TILE, TILE)] if here == 0 and column == 0 else spot(here, column, tile)
        return pltpu.make_async_remote_copy(
            src_ref=source,
            dst_ref=spot(-sign * step, column, tile),
            send_sem=send_sem.at[index],
            recv_sem=recv_sem.at[index],
            device_id=ring[way],
            device_id_type=MESH,
        )

    def mate_copy(offset, tile):
        offset = depth - half if offset == -half else offset
        index = 6 * half + offset + half - 1
        if tile:
            index = 7 * half + depth // 2
            if offset:
                index += 1 + 2 * BY_MATE.index(abs(offset)) + (offset > 0)
        source = feat.at[pl.ds(tile * TILE, TILE)] if offset == 0 else spot(offset, 0, tile)
        return pltpu.make_async_remote_copy(
            src_ref=source,
            dst_ref=spot(offset, 1, tile),
            send_sem=send_sem.at[index],
            recv_sem=recv_sem.at[index],
            device_id=mate,
            device_id_type=MESH,
        )

    def begin(copy):
        copy.start()
        started.append(copy)

    positions = lax.broadcasted_iota(jnp.int32, (TILE, rows_ref.shape[1]), 0)
    lanes = lax.broadcasted_iota(jnp.int32, (1, rows_ref.shape[1]), 1)

    def build_mats(first, stop):
        def body(i, carry):
            live = jnp.where(lanes < counts[0, i], strength[pl.ds(i, 1), :], 0.0)
            at_row = jnp.where(positions == rows_ref[pl.ds(i, 1), :], 1.0, 0.0).astype(jnp.bfloat16)
            at_col = jnp.where(positions == cols_ref[pl.ds(i, 1), :], live, 0.0).astype(jnp.bfloat16)
            mats_v[i] = lax.dot_general(
                at_row, at_col, (((1,), (1,)), ((), ())), preferred_element_type=jnp.float32
            ).astype(jnp.bfloat16)
            return carry

        lax.fori_loop(first, stop, body, 0)

    chunk = 256
    chunks = acc_v.shape[0] // chunk

    def dense_part(first, stop):
        def body(i, carry):
            rows = pl.ds(pl.multiple_of(i * chunk, chunk), chunk)
            both = jnp.dot(
                dense_v[rows].reshape(2 * chunk, FEAT), panels[...], preferred_element_type=jnp.float32
            )
            for lane in range(4):
                mixed[lane] = both[:, lane * TILE : (lane + 1) * TILE]
            for lane in range(2):
                acc_v[rows, pl.ds(lane * TILE, TILE)] = (
                    mixed[lane, pl.ds(0, chunk, stride=2), :] + mixed[lane + 2, pl.ds(1, chunk, stride=2), :]
                )
            return carry

        lax.fori_loop(first, stop, body, 0)

    def fetch_panels():
        for slot in range(2):
            label = labels[0, slot]
            wanted = lax.rem(label // 2 - z + NEAR + depth, depth) * 2 + lax.rem(label + side, 2)
            first = 2 * (half - 1 - NEAR)
            panel = got[first]
            for k in range(1, 2 * (2 * NEAR + 1)):
                panel = jnp.where(wanted == k, got[first + k], panel)
            panels[:, pl.ds(slot * FEAT, FEAT)] = panel

    begin(mate_copy(0, 1))
    for piece in (0, 1):
        for way in (0, 1):
            begin(ring_copy(piece, way, 1))
    begin(mate_copy(0, 0))
    mate_copy(0, 1).wait_recv()
    for way in (0, 1):
        begin(ring_copy(2, way, 1))

    tiles = mats_v.shape[0]
    early = 2 * half
    late = half
    slot = 0
    for step in range(1, half + 1):
        for piece in range(3):
            if slot < early:
                build_mats(slot * tiles // early, (slot + 1) * tiles // early)
            else:
                if slot == early:
                    mate_copy(0, 0).wait_recv()
                    for near_step in range(1, NEAR + 1):
                        for sign in step_sign:
                            mate_copy(-sign * near_step, 0).wait_recv()
                    fetch_panels()
                    dense_in.wait()
                dense_part((slot - early) * chunks // late, (slot - early + 1) * chunks // late)
            for way in (0, 1):
                if step <= last[piece][way]:
                    away = -step_sign[way] * step
                    if piece == 2 and step in BY_MATE:
                        mate_copy(away, 1).wait_recv()
                    else:
                        ring_copy(piece, way, step).wait_recv()
                    if step < last[piece][way] and not (piece == 2 and step + 1 in BY_MATE):
                        begin(ring_copy(piece, way, step + 1))
                    if piece == 0 or piece == 1 and step in BY_MATE:
                        begin(mate_copy(away, piece))
            slot += 1
    for offset in range(NEAR + 1, half + 1):
        mate_copy(offset, 0).wait_recv()
        if offset < half:
            mate_copy(-offset, 0).wait_recv()
    for copy in started:
        copy.wait_send()


def gather_and_prepare(features, dense_blocks, labels, counts, rows, cols, strength):
    depth = lax.axis_size("row") // 2
    block_rows = dense_blocks.shape[0]
    tiles = rows.shape[0]
    sems = 3 * depth + depth + 1 + 2 * len(BY_MATE)
    vmem = pl.BlockSpec(memory_space=pltpu.VMEM)
    smem = pl.BlockSpec(memory_space=pltpu.SMEM)
    return pl.pallas_call(
        functools.partial(gather_kernel, depth),
        out_shape=(
            pltpu.VMEM((2 * depth, FEAT, FEAT), jnp.bfloat16),
            pltpu.VMEM((block_rows, FEAT), jnp.float32),
            pltpu.VMEM((tiles, TILE, TILE), jnp.bfloat16),
        ),
        in_specs=[smem, smem, vmem, vmem, vmem, vmem, pl.BlockSpec(memory_space=pl.ANY)],
        out_specs=(vmem, vmem, vmem),
        scratch_shapes=[
            pltpu.VMEM((FEAT, 2 * FEAT), jnp.bfloat16),
            pltpu.VMEM((4, 2 * FEAT, TILE), jnp.float32),
            pltpu.VMEM(rows.shape, jnp.float32),
            pltpu.VMEM(dense_blocks.shape, jnp.bfloat16),
            pltpu.SemaphoreType.DMA((sems,)),
            pltpu.SemaphoreType.DMA((sems,)),
            pltpu.SemaphoreType.DMA,
        ],
        compiler_params=pltpu.CompilerParams(collective_id=0, has_side_effects=True, vmem_limit_bytes=67043328 - 10 * 2**20 - 65536),
        name="gather_and_prepare",
    )(labels, counts, features, rows, cols, strength, dense_blocks)


def place_kernel(depth, source, dest, got, mats, dense, out, acc):
    acc[...] = jnp.zeros_like(acc)
    me = lax.axis_index("row")
    half = depth // 2
    group = 4

    def spot(i):
        listed = source[0, i]
        block = lax.div(listed, 2)
        offset = lax.rem(lax.div(block, 2) - lax.div(me, 2) + half - 1 + depth, depth)
        return (offset * 2 + lax.rem(block + me, 2)) * 2 + lax.rem(listed, 2)

    def body(g, carry):
        terms = [
            jnp.dot(
                mats[g * group + k], got[spot(g * group + k)], preferred_element_type=jnp.float32
            )
            for k in range(group)
        ]
        for k in range(group):
            rows = pl.ds(pl.multiple_of(dest[0, g * group + k] * TILE, TILE), TILE)
            acc[rows, :] += terms[k]
        return carry

    lax.fori_loop(0, mats.shape[0] // group, body, 0)
    out[...] = (acc[...] + dense[...]).astype(jnp.bfloat16)


def place_tiles(source, dest, got, mats, acc):
    vmem = pl.BlockSpec(memory_space=pltpu.VMEM)
    smem = pl.BlockSpec(memory_space=pltpu.SMEM)
    return pl.pallas_call(
        functools.partial(place_kernel, lax.axis_size("row") // 2),
        out_shape=jax.ShapeDtypeStruct(acc.shape, jnp.bfloat16),
        in_specs=[smem, smem, vmem, vmem, vmem],
        out_specs=vmem,
        scratch_shapes=[pltpu.VMEM(acc.shape, jnp.float32)],
        compiler_params=pltpu.CompilerParams(vmem_limit_bytes=20 * 2**20),
        name="place_tiles",
    )(source, dest, got, mats, acc)


def scatter_kernel(
    part, weight, bias, out, from_core, sum_core, from_one, sum_one, from_two, sum_two, from_x, send_sem, recv_sem
):
    me = lax.axis_index("rep")
    core = me % 2
    y = (me // 2) % 4
    x = me // 8

    def rep_of(xx, yy, cc):
        return (xx * 4 + yy) * 2 + cc

    flips = (y, y + 1 - 2 * (y % 2), (y + 2) % 4, 3 - y)
    mate = {"rep": rep_of(x, y, 1 - core)}
    y_peer = {1: {"rep": rep_of(x, flips[1], core)}, 3: {"rep": rep_of(x, flips[3], core)}}
    x_peer = {"rep": rep_of(1 - x, y, core)}
    barrier = pltpu.get_barrier_semaphore()
    for peer in (mate, y_peer[1], y_peer[3], x_peer):
        pl.semaphore_signal(barrier, inc=1, device_id=peer, device_id_type=MESH)
    pl.semaphore_wait(barrier, 4)

    def piece(h, q, t, cc):
        xx = x if q == 0 else 1 - x
        first = rep_of(xx, flips[t], cc) * (2 * TILE) + h * TILE
        return part.at[pl.ds(pl.multiple_of(first, TILE), TILE)]

    def number(h, q, t):
        return (h * 2 + q) * 4 + t

    def remote(source, target, index, peer):
        return pltpu.make_async_remote_copy(
            src_ref=source,
            dst_ref=target,
            send_sem=send_sem.at[index],
            recv_sem=recv_sem.at[index],
            device_id=peer,
            device_id_type=MESH,
        )

    def core_copy(h, q, t):
        n = number(h, q, t)
        return remote(piece(h, q, t, 1 - core), from_core.at[n], n, mate)

    def one_copy(h, q, t):
        way = HALVES[h][0]
        arrives = {1: {1: 0, 2: 3}, 3: {3: 0, 2: 1}}[way][t]
        slot = (h * 2 + q) * 2 + (0 if arrives == 0 else 1)
        return remote(sum_core.at[slot], from_one.at[slot], 16 + slot, y_peer[way])

    def two_copy(h, q):
        slot = h * 2 + q
        return remote(sum_two.at[slot], from_two.at[slot], 24 + slot, y_peer[HALVES[h][1]])

    def x_copy(h):
        return remote(sum_one.at[h], from_x.at[h], 28 + h, x_peer)

    def wide(ref):
        return ref[...].astype(jnp.float32)

    started = []

    def begin(copy):
        copy.start()
        started.append(copy)

    first_order = [(h, q, t) for t in (0, 1) for q in (1, 0) for h in (0, 1)]
    sends_one = [(h, q, 2 if k == 0 else HALVES[h][0]) for (h, q, k) in first_order]
    stays = [(h, q, HALVES[h][1]) for q in (1, 0) for h in (0, 1)]
    ends = [(h, q, 0) for q in (1, 0) for h in (0, 1)]
    for key in sends_one + stays + ends:
        begin(core_copy(*key))
    for h, q, t in sends_one:
        copy = one_copy(h, q, t)
        core_copy(h, q, t).wait_recv()
        way = HALVES[h][0]
        slot = (h * 2 + q) * 2 + (0 if t == way else 1)
        sum_core[slot] = (
            wide(piece(h, q, t, core)) + wide(from_core.at[number(h, q, t)])
        ).astype(jnp.bfloat16)
        begin(copy)
    for h, q, t in stays:
        core_copy(h, q, t).wait_recv()
        one_copy(h, q, 2).wait_recv()
        sum_two[h * 2 + q] = (
            wide(piece(h, q, t, core))
            + wide(from_core.at[number(h, q, t)])
            + wide(from_one.at[(h * 2 + q) * 2 + 1])
        ).astype(jnp.bfloat16)
        begin(two_copy(h, q))

    def total(h, q):
        core_copy(h, q, 0).wait_recv()
        one_copy(h, q, HALVES[h][0]).wait_recv()
        two_copy(h, q).wait_recv()
        return (
            wide(piece(h, q, 0, core))
            + wide(from_core.at[number(h, q, 0)])
            + wide(from_one.at[(h * 2 + q) * 2])
            + wide(from_two.at[h * 2 + q])
        )

    for h in (0, 1):
        sum_one[h] = total(h, 1).astype(jnp.bfloat16)
        begin(x_copy(h))
    for h in (0, 1):
        own = total(h, 0)
        x_copy(h).wait_recv()
        hidden = (own + wide(from_x.at[h])).astype(jnp.bfloat16)
        projected = jnp.dot(hidden, weight[...], preferred_element_type=jnp.float32) + bias[...]
        out[pl.ds(h * TILE, TILE), :] = jnp.maximum(projected, 0.0).astype(jnp.bfloat16)
    for copy in started:
        copy.wait_send()


def scatter_and_project(part, weight, bias):
    vmem = pl.BlockSpec(memory_space=pltpu.VMEM)

    def tiles(n):
        return pltpu.VMEM((n, TILE, FEAT), jnp.bfloat16)

    return pl.pallas_call(
        scatter_kernel,
        out_shape=jax.ShapeDtypeStruct((2 * TILE, FEAT), jnp.bfloat16),
        in_specs=[vmem, vmem, vmem],
        out_specs=vmem,
        scratch_shapes=[
            tiles(16),
            tiles(8),
            tiles(8),
            tiles(2),
            tiles(4),
            tiles(4),
            tiles(2),
            pltpu.SemaphoreType.DMA((30,)),
            pltpu.SemaphoreType.DMA((30,)),
        ],
        compiler_params=pltpu.CompilerParams(collective_id=1, has_side_effects=True, vmem_limit_bytes=10 * 2**20),
        name="scatter_and_project",
    )(part, weight, bias)


def shards(
    features,
    dense_blocks,
    thick_neighbour_labels,
    tile_source,
    tile_dest,
    entry_rows,
    entry_cols,
    edge_strength_list,
    entry_count,
    weight,
    out_bias,
):
    depth = lax.axis_size("row") // 2
    got, acc, mats = gather_and_prepare(
        features,
        dense_blocks,
        thick_neighbour_labels,
        entry_count[0],
        entry_rows[0, 0],
        entry_cols[0, 0],
        edge_strength_list[0, 0],
    )
    part = place_tiles(
        tile_source[0],
        tile_dest[0],
        got.reshape(4 * depth, TILE, FEAT),
        mats,
        acc,
    )
    return scatter_and_project(part, weight, out_bias.reshape(1, FEAT))


def solution(mesh):
    return jax.shard_map(
        shards,
        mesh=mesh,
        in_specs=(
            P(("row", "rep"), None),
            P("row", None, "rep"),
            P("row", None),
            P("row", "rep", None),
            P("row", "rep", None),
            P("row", "rep", None, None),
            P("row", "rep", None, None),
            P("row", "rep", None, None),
            P("row", "rep", None),
            P(),
            P(),
        ),
        out_specs=P(("row", "rep"), None),
        check_vma=False,
    )
```

```python
import functools

import jax
import jax.numpy as jnp
from jax import lax
from jax.experimental import pallas as pl
from jax.experimental.pallas import tpu as pltpu
from jax.sharding import PartitionSpec as P

FEAT = 256
TILE = 128
NEAR = 2
BY_MATE = (4, 6)
MESH = pl.DeviceIdType.MESH
HALVES = ((1, 3), (3, 1))


def gather_kernel(
    depth,
    labels,
    counts,
    feat,
    rows_ref,
    cols_ref,
    strength_in,
    dense_hbm,
    got,
    acc_v,
    mats_v,
    panels,
    mixed,
    strength,
    dense_v,
    send_sem,
    recv_sem,
    local_sem,
):
    me = lax.axis_index("row")
    z = me // 2
    side = me % 2
    mate = {"row": z * 2 + 1 - side}
    ring = (
        {"row": lax.rem(z + 1, depth) * 2 + side},
        {"row": lax.rem(z + depth - 1, depth) * 2 + side},
    )
    step_sign = (1, -1)
    half = depth // 2

    barrier = pltpu.get_barrier_semaphore()
    for peer in (mate,) + ring:
        pl.semaphore_signal(barrier, inc=1, device_id=peer, device_id_type=MESH)

    dense_in = pltpu.make_async_copy(dense_hbm, dense_v, local_sem)
    dense_in.start()
    got[2 * (half - 1)] = feat[...]
    strength[...] = strength_in[...].astype(jnp.float32)
    pl.semaphore_wait(barrier, 3)

    def spot(offset, column, tile):
        rows = pl.ds(tile * TILE, TILE)
        offset = depth - half if offset == -half else offset
        return got.at[(offset + half - 1) * 2 + column, rows]

    pieces = ((0, 0), (0, 1), (1, 1))
    last = ((half, half - 1), (half - 1, half), (half, half - 1))
    started = []

    def ring_copy(piece, way, step):
        column, tile = pieces[piece]
        sign = step_sign[way]
        here = -sign * (step - 1)
        index = (piece * 2 + way) * half + step - 1
        source = feat.at[pl.ds(tile * TILE, TILE)] if here == 0 and column == 0 else spot(here, column, tile)
        return pltpu.make_async_remote_copy(
            src_ref=source,
            dst_ref=spot(-sign * step, column, tile),
            send_sem=send_sem.at[index],
            recv_sem=recv_sem.at[index],
            device_id=ring[way],
            device_id_type=MESH,
        )

    def mate_copy(offset, tile):
        offset = depth - half if offset == -half else offset
        index = 6 * half + offset + half - 1
        if tile:
            index = 7 * half + depth // 2
            if offset:
                index += 1 + 2 * BY_MATE.index(abs(offset)) + (offset > 0)
        source = feat.at[pl.ds(tile * TILE, TILE)] if offset == 0 else spot(offset, 0, tile)
        return pltpu.make_async_remote_copy(
            src_ref=source,
            dst_ref=spot(offset, 1, tile),
            send_sem=send_sem.at[index],
            recv_sem=recv_sem.at[index],
            device_id=mate,
            device_id_type=MESH,
        )

    def begin(copy):
        copy.start()
        started.append(copy)

    positions = lax.broadcasted_iota(jnp.int32, (TILE, rows_ref.shape[1]), 0)
    lanes = lax.broadcasted_iota(jnp.int32, (1, rows_ref.shape[1]), 1)

    def build_mats(first, stop):
        def body(i, carry):
            live = jnp.where(lanes < counts[0, i], strength[pl.ds(i, 1), :], 0.0)
            at_row = jnp.where(positions == rows_ref[pl.ds(i, 1), :], 1.0, 0.0).astype(jnp.bfloat16)
            at_col = jnp.where(positions == cols_ref[pl.ds(i, 1), :], live, 0.0).astype(jnp.bfloat16)
            mats_v[i] = lax.dot_general(
                at_row, at_col, (((1,), (1,)), ((), ())), preferred_element_type=jnp.float32
            ).astype(jnp.bfloat16)
            return carry

        lax.fori_loop(first, stop, body, 0)

    chunk = 256
    chunks = acc_v.shape[0] // chunk

    def dense_part(first, stop):
        def body(i, carry):
            rows = pl.ds(pl.multiple_of(i * chunk, chunk), chunk)
            both = jnp.dot(
                dense_v[rows].reshape(2 * chunk, FEAT), panels[...], preferred_element_type=jnp.float32
            )
            for lane in range(4):
                mixed[lane] = both[:, lane * TILE : (lane + 1) * TILE]
            for lane in range(2):
                acc_v[rows, pl.ds(lane * TILE, TILE)] = (
                    mixed[lane, pl.ds(0, chunk, stride=2), :] + mixed[lane + 2, pl.ds(1, chunk, stride=2), :]
                )
            return carry

        lax.fori_loop(first, stop, body, 0)

    def fetch_panels():
        for slot in range(2):
            label = labels[0, slot]
            wanted = lax.rem(label // 2 - z + NEAR + depth, depth) * 2 + lax.rem(label + side, 2)
            first = 2 * (half - 1 - NEAR)
            panel = got[first]
            for k in range(1, 2 * (2 * NEAR + 1)):
                panel = jnp.where(wanted == k, got[first + k], panel)
            panels[:, pl.ds(slot * FEAT, FEAT)] = panel

    begin(mate_copy(0, 1))
    for piece in (0, 1):
        for way in (0, 1):
            begin(ring_copy(piece, way, 1))
    begin(mate_copy(0, 0))
    mate_copy(0, 1).wait_recv()
    for way in (0, 1):
        begin(ring_copy(2, way, 1))

    tiles = mats_v.shape[0]
    early = 2 * half
    late = half
    slot = 0
    for step in range(1, half + 1):
        for piece in range(3):
            if slot < early:
                build_mats(slot * tiles // early, (slot + 1) * tiles // early)
            else:
                if slot == early:
                    mate_copy(0, 0).wait_recv()
                    for near_step in range(1, NEAR + 1):
                        for sign in step_sign:
                            mate_copy(-sign * near_step, 0).wait_recv()
                    fetch_panels()
                    dense_in.wait()
                dense_part((slot - early) * chunks // late, (slot - early + 1) * chunks // late)
            for way in (0, 1):
                if step <= last[piece][way]:
                    if piece == 2 and step in BY_MATE:
                        continue
                    away = -step_sign[way] * step
                    ring_copy(piece, way, step).wait_recv()
                    if step < last[piece][way] and not (piece == 2 and step + 1 in BY_MATE):
                        begin(ring_copy(piece, way, step + 1))
                    if piece == 0 or piece == 1 and step in BY_MATE:
                        begin(mate_copy(away, piece))
            if piece == 0 and step - 1 in BY_MATE:
                for way in (0, 1):
                    mate_copy(-step_sign[way] * (step - 1), 1).wait_recv()
                    begin(ring_copy(2, way, step))
            slot += 1
    for offset in range(NEAR + 1, half + 1):
        mate_copy(offset, 0).wait_recv()
        if offset < half:
            mate_copy(-offset, 0).wait_recv()
    for copy in started:
        copy.wait_send()


def gather_and_prepare(features, dense_blocks, labels, counts, rows, cols, strength):
    depth = lax.axis_size("row") // 2
    block_rows = dense_blocks.shape[0]
    tiles = rows.shape[0]
    sems = 3 * depth + depth + 1 + 2 * len(BY_MATE)
    vmem = pl.BlockSpec(memory_space=pltpu.VMEM)
    smem = pl.BlockSpec(memory_space=pltpu.SMEM)
    return pl.pallas_call(
        functools.partial(gather_kernel, depth),
        out_shape=(
            pltpu.VMEM((2 * depth, FEAT, FEAT), jnp.bfloat16),
            pltpu.VMEM((block_rows, FEAT), jnp.float32),
            pltpu.VMEM((tiles, TILE, TILE), jnp.bfloat16),
        ),
        in_specs=[smem, smem, vmem, vmem, vmem, vmem, pl.BlockSpec(memory_space=pl.ANY)],
        out_specs=(vmem, vmem, vmem),
        scratch_shapes=[
            pltpu.VMEM((FEAT, 2 * FEAT), jnp.bfloat16),
            pltpu.VMEM((4, 2 * FEAT, TILE), jnp.float32),
            pltpu.VMEM(rows.shape, jnp.float32),
            pltpu.VMEM(dense_blocks.shape, jnp.bfloat16),
            pltpu.SemaphoreType.DMA((sems,)),
            pltpu.SemaphoreType.DMA((sems,)),
            pltpu.SemaphoreType.DMA,
        ],
        compiler_params=pltpu.CompilerParams(collective_id=0, has_side_effects=True, vmem_limit_bytes=67043328 - 10 * 2**20 - 65536),
        name="gather_and_prepare",
    )(labels, counts, features, rows, cols, strength, dense_blocks)


def place_kernel(depth, source, dest, got, mats, dense, out, acc):
    acc[...] = jnp.zeros_like(acc)
    me = lax.axis_index("row")
    half = depth // 2
    group = 4

    def spot(i):
        listed = source[0, i]
        block = lax.div(listed, 2)
        offset = lax.rem(lax.div(block, 2) - lax.div(me, 2) + half - 1 + depth, depth)
        return (offset * 2 + lax.rem(block + me, 2)) * 2 + lax.rem(listed, 2)

    def body(g, carry):
        terms = [
            jnp.dot(
                mats[g * group + k], got[spot(g * group + k)], preferred_element_type=jnp.float32
            )
            for k in range(group)
        ]
        for k in range(group):
            rows = pl.ds(pl.multiple_of(dest[0, g * group + k] * TILE, TILE), TILE)
            acc[rows, :] += terms[k]
        return carry

    lax.fori_loop(0, mats.shape[0] // group, body, 0)
    out[...] = (acc[...] + dense[...]).astype(jnp.bfloat16)


def place_tiles(source, dest, got, mats, acc):
    vmem = pl.BlockSpec(memory_space=pltpu.VMEM)
    smem = pl.BlockSpec(memory_space=pltpu.SMEM)
    return pl.pallas_call(
        functools.partial(place_kernel, lax.axis_size("row") // 2),
        out_shape=jax.ShapeDtypeStruct(acc.shape, jnp.bfloat16),
        in_specs=[smem, smem, vmem, vmem, vmem],
        out_specs=vmem,
        scratch_shapes=[pltpu.VMEM(acc.shape, jnp.float32)],
        compiler_params=pltpu.CompilerParams(vmem_limit_bytes=20 * 2**20),
        name="place_tiles",
    )(source, dest, got, mats, acc)


def scatter_kernel(
    part, weight, bias, out, from_core, sum_core, from_one, sum_one, from_two, sum_two, from_x, send_sem, recv_sem
):
    me = lax.axis_index("rep")
    core = me % 2
    y = (me // 2) % 4
    x = me // 8

    def rep_of(xx, yy, cc):
        return (xx * 4 + yy) * 2 + cc

    flips = (y, y + 1 - 2 * (y % 2), (y + 2) % 4, 3 - y)
    mate = {"rep": rep_of(x, y, 1 - core)}
    y_peer = {1: {"rep": rep_of(x, flips[1], core)}, 3: {"rep": rep_of(x, flips[3], core)}}
    x_peer = {"rep": rep_of(1 - x, y, core)}
    barrier = pltpu.get_barrier_semaphore()
    for peer in (mate, y_peer[1], y_peer[3], x_peer):
        pl.semaphore_signal(barrier, inc=1, device_id=peer, device_id_type=MESH)
    pl.semaphore_wait(barrier, 4)

    def piece(h, q, t, cc):
        xx = x if q == 0 else 1 - x
        first = rep_of(xx, flips[t], cc) * (2 * TILE) + h * TILE
        return part.at[pl.ds(pl.multiple_of(first, TILE), TILE)]

    def number(h, q, t):
        return (h * 2 + q) * 4 + t

    def remote(source, target, index, peer):
        return pltpu.make_async_remote_copy(
            src_ref=source,
            dst_ref=target,
            send_sem=send_sem.at[index],
            recv_sem=recv_sem.at[index],
            device_id=peer,
            device_id_type=MESH,
        )

    def core_copy(h, q, t):
        n = number(h, q, t)
        return remote(piece(h, q, t, 1 - core), from_core.at[n], n, mate)

    def one_copy(h, q, t):
        way = HALVES[h][0]
        arrives = {1: {1: 0, 2: 3}, 3: {3: 0, 2: 1}}[way][t]
        slot = (h * 2 + q) * 2 + (0 if arrives == 0 else 1)
        return remote(sum_core.at[slot], from_one.at[slot], 16 + slot, y_peer[way])

    def two_copy(h, q):
        slot = h * 2 + q
        return remote(sum_two.at[slot], from_two.at[slot], 24 + slot, y_peer[HALVES[h][1]])

    def x_copy(h):
        return remote(sum_one.at[h], from_x.at[h], 28 + h, x_peer)

    def wide(ref):
        return ref[...].astype(jnp.float32)

    started = []

    def begin(copy):
        copy.start()
        started.append(copy)

    def send_one(h, q, t):
        copy = one_copy(h, q, t)
        core_copy(h, q, t).wait_recv()
        slot = (h * 2 + q) * 2 + (0 if t == HALVES[h][0] else 1)
        sum_core[slot] = (
            wide(piece(h, q, t, core)) + wide(from_core.at[number(h, q, t)])
        ).astype(jnp.bfloat16)
        begin(copy)

    def send_two(h, q, t):
        core_copy(h, q, t).wait_recv()
        one_copy(h, q, 2).wait_recv()
        sum_two[h * 2 + q] = (
            wide(piece(h, q, t, core))
            + wide(from_core.at[number(h, q, t)])
            + wide(from_one.at[(h * 2 + q) * 2 + 1])
        ).astype(jnp.bfloat16)
        begin(two_copy(h, q))

    plan = []
    for send, q, place in (
        (send_one, 1, None),
        (send_one, 1, 0),
        (send_one, 0, None),
        (send_two, 1, 1),
        (send_one, 0, 0),
        (send_two, 0, 1),
    ):
        for h in (0, 1):
            plan.append((send, (h, q, 2 if place is None else HALVES[h][place])))
    for send, key in plan:
        begin(core_copy(*key))
    for q in (1, 0):
        for h in (0, 1):
            begin(core_copy(h, q, 0))
    for send, key in plan:
        send(*key)

    def total(h, q):
        core_copy(h, q, 0).wait_recv()
        one_copy(h, q, HALVES[h][0]).wait_recv()
        two_copy(h, q).wait_recv()
        return (
            wide(piece(h, q, 0, core))
            + wide(from_core.at[number(h, q, 0)])
            + wide(from_one.at[(h * 2 + q) * 2])
            + wide(from_two.at[h * 2 + q])
        )

    for h in (0, 1):
        sum_one[h] = total(h, 1).astype(jnp.bfloat16)
        begin(x_copy(h))
    for h in (0, 1):
        own = total(h, 0)
        x_copy(h).wait_recv()
        hidden = (own + wide(from_x.at[h])).astype(jnp.bfloat16)
        projected = jnp.dot(hidden, weight[...], preferred_element_type=jnp.float32) + bias[...]
        out[pl.ds(h * TILE, TILE), :] = jnp.maximum(projected, 0.0).astype(jnp.bfloat16)
    for copy in started:
        copy.wait_send()


def scatter_and_project(part, weight, bias):
    vmem = pl.BlockSpec(memory_space=pltpu.VMEM)

    def tiles(n):
        return pltpu.VMEM((n, TILE, FEAT), jnp.bfloat16)

    return pl.pallas_call(
        scatter_kernel,
        out_shape=jax.ShapeDtypeStruct((2 * TILE, FEAT), jnp.bfloat16),
        in_specs=[vmem, vmem, vmem],
        out_specs=vmem,
        scratch_shapes=[
            tiles(16),
            tiles(8),
            tiles(8),
            tiles(2),
            tiles(4),
            tiles(4),
            tiles(2),
            pltpu.SemaphoreType.DMA((30,)),
            pltpu.SemaphoreType.DMA((30,)),
        ],
        compiler_params=pltpu.CompilerParams(collective_id=1, has_side_effects=True, vmem_limit_bytes=10 * 2**20),
        name="scatter_and_project",
    )(part, weight, bias)


def shards(
    features,
    dense_blocks,
    thick_neighbour_labels,
    tile_source,
    tile_dest,
    entry_rows,
    entry_cols,
    edge_strength_list,
    entry_count,
    weight,
    out_bias,
):
    depth = lax.axis_size("row") // 2
    got, acc, mats = gather_and_prepare(
        features,
        dense_blocks,
        thick_neighbour_labels,
        entry_count[0],
        entry_rows[0, 0],
        entry_cols[0, 0],
        edge_strength_list[0, 0],
    )
    part = place_tiles(
        tile_source[0],
        tile_dest[0],
        got.reshape(4 * depth, TILE, FEAT),
        mats,
        acc,
    )
    return scatter_and_project(part, weight, out_bias.reshape(1, FEAT))


def solution(mesh):
    return jax.shard_map(
        shards,
        mesh=mesh,
        in_specs=(
            P(("row", "rep"), None),
            P("row", None, "rep"),
            P("row", None),
            P("row", "rep", None),
            P("row", "rep", None),
            P("row", "rep", None, None),
            P("row", "rep", None, None),
            P("row", "rep", None, None),
            P("row", "rep", None),
            P(),
            P(),
        ),
        out_specs=P(("row", "rep"), None),
        check_vma=False,
    )
```

```python
import functools

import jax
import jax.numpy as jnp
from jax import lax
from jax.experimental import pallas as pl
from jax.experimental.pallas import tpu as pltpu
from jax.sharding import PartitionSpec as P

FEAT = 256
TILE = 128
NEAR = 2
BY_MATE = (5,)
MESH = pl.DeviceIdType.MESH
HALVES = ((1, 3), (3, 1))


def gather_kernel(
    depth,
    labels,
    counts,
    feat,
    rows_ref,
    cols_ref,
    strength_in,
    dense_hbm,
    got,
    acc_v,
    mats_v,
    panels,
    mixed,
    strength,
    dense_v,
    send_sem,
    recv_sem,
    local_sem,
):
    me = lax.axis_index("row")
    z = me // 2
    side = me % 2
    mate = {"row": z * 2 + 1 - side}
    ring = (
        {"row": lax.rem(z + 1, depth) * 2 + side},
        {"row": lax.rem(z + depth - 1, depth) * 2 + side},
    )
    step_sign = (1, -1)
    half = depth // 2

    barrier = pltpu.get_barrier_semaphore()
    for peer in (mate,) + ring:
        pl.semaphore_signal(barrier, inc=1, device_id=peer, device_id_type=MESH)

    dense_in = pltpu.make_async_copy(dense_hbm, dense_v, local_sem)
    dense_in.start()
    got[2 * (half - 1)] = feat[...]
    strength[...] = strength_in[...].astype(jnp.float32)
    pl.semaphore_wait(barrier, 3)

    def spot(offset, column, tile):
        rows = pl.ds(tile * TILE, TILE)
        offset = depth - half if offset == -half else offset
        return got.at[(offset + half - 1) * 2 + column, rows]

    pieces = ((0, 0), (0, 1), (1, 1))
    last = ((half, half - 1), (half - 1, half), (half, half - 1))
    started = []

    def ring_copy(piece, way, step):
        column, tile = pieces[piece]
        sign = step_sign[way]
        here = -sign * (step - 1)
        index = (piece * 2 + way) * half + step - 1
        source = feat.at[pl.ds(tile * TILE, TILE)] if here == 0 and column == 0 else spot(here, column, tile)
        return pltpu.make_async_remote_copy(
            src_ref=source,
            dst_ref=spot(-sign * step, column, tile),
            send_sem=send_sem.at[index],
            recv_sem=recv_sem.at[index],
            device_id=ring[way],
            device_id_type=MESH,
        )

    def mate_copy(offset, tile):
        offset = depth - half if offset == -half else offset
        index = 6 * half + offset + half - 1
        if tile:
            index = 7 * half + depth // 2
            if offset:
                index += 1 + 2 * BY_MATE.index(abs(offset)) + (offset > 0)
        source = feat.at[pl.ds(tile * TILE, TILE)] if offset == 0 else spot(offset, 0, tile)
        return pltpu.make_async_remote_copy(
            src_ref=source,
            dst_ref=spot(offset, 1, tile),
            send_sem=send_sem.at[index],
            recv_sem=recv_sem.at[index],
            device_id=mate,
            device_id_type=MESH,
        )

    def begin(copy):
        copy.start()
        started.append(copy)

    positions = lax.broadcasted_iota(jnp.int32, (TILE, rows_ref.shape[1]), 0)
    lanes = lax.broadcasted_iota(jnp.int32, (1, rows_ref.shape[1]), 1)

    def build_mats(first, stop):
        def body(i, carry):
            live = jnp.where(lanes < counts[0, i], strength[pl.ds(i, 1), :], 0.0)
            at_row = jnp.where(positions == rows_ref[pl.ds(i, 1), :], 1.0, 0.0).astype(jnp.bfloat16)
            at_col = jnp.where(positions == cols_ref[pl.ds(i, 1), :], live, 0.0).astype(jnp.bfloat16)
            mats_v[i] = lax.dot_general(
                at_row, at_col, (((1,), (1,)), ((), ())), preferred_element_type=jnp.float32
            ).astype(jnp.bfloat16)
            return carry

        lax.fori_loop(first, stop, body, 0)

    chunk = 256
    chunks = acc_v.shape[0] // chunk

    def dense_part(first, stop):
        def body(i, carry):
            rows = pl.ds(pl.multiple_of(i * chunk, chunk), chunk)
            both = jnp.dot(
                dense_v[rows].reshape(2 * chunk, FEAT), panels[...], preferred_element_type=jnp.float32
            )
            for lane in range(4):
                mixed[lane] = both[:, lane * TILE : (lane + 1) * TILE]
            for lane in range(2):
                acc_v[rows, pl.ds(lane * TILE, TILE)] = (
                    mixed[lane, pl.ds(0, chunk, stride=2), :] + mixed[lane + 2, pl.ds(1, chunk, stride=2), :]
                )
            return carry

        lax.fori_loop(first, stop, body, 0)

    def fetch_panels():
        for slot in range(2):
            label = labels[0, slot]
            wanted = lax.rem(label // 2 - z + NEAR + depth, depth) * 2 + lax.rem(label + side, 2)
            first = 2 * (half - 1 - NEAR)
            panel = got[first]
            for k in range(1, 2 * (2 * NEAR + 1)):
                panel = jnp.where(wanted == k, got[first + k], panel)
            panels[:, pl.ds(slot * FEAT, FEAT)] = panel

    begin(mate_copy(0, 1))
    for piece in (0, 1):
        for way in (0, 1):
            begin(ring_copy(piece, way, 1))
    begin(mate_copy(0, 0))
    mate_copy(0, 1).wait_recv()
    for way in (0, 1):
        begin(ring_copy(2, way, 1))

    tiles = mats_v.shape[0]
    early = 2 * half
    late = half
    slot = 0
    for step in range(1, half + 1):
        for piece in range(3):
            if slot < early:
                build_mats(slot * tiles // early, (slot + 1) * tiles // early)
            else:
                if slot == early:
                    mate_copy(0, 0).wait_recv()
                    for near_step in range(1, NEAR + 1):
                        for sign in step_sign:
                            mate_copy(-sign * near_step, 0).wait_recv()
                    fetch_panels()
                    dense_in.wait()
                dense_part((slot - early) * chunks // late, (slot - early + 1) * chunks // late)
            for way in (0, 1):
                if step <= last[piece][way]:
                    if piece == 2 and step in BY_MATE:
                        continue
                    away = -step_sign[way] * step
                    ring_copy(piece, way, step).wait_recv()
                    if step < last[piece][way] and not (piece == 2 and step + 1 in BY_MATE):
                        begin(ring_copy(piece, way, step + 1))
                    if piece == 0 or piece == 1 and step in BY_MATE:
                        begin(mate_copy(away, piece))
            if piece == 0 and step - 1 in BY_MATE:
                for way in (0, 1):
                    mate_copy(-step_sign[way] * (step - 1), 1).wait_recv()
                    begin(ring_copy(2, way, step))
            slot += 1
    for offset in range(NEAR + 1, half + 1):
        mate_copy(offset, 0).wait_recv()
        if offset < half:
            mate_copy(-offset, 0).wait_recv()
    for copy in started:
        copy.wait_send()


def gather_and_prepare(features, dense_blocks, labels, counts, rows, cols, strength):
    depth = lax.axis_size("row") // 2
    block_rows = dense_blocks.shape[0]
    tiles = rows.shape[0]
    sems = 3 * depth + depth + 1 + 2 * len(BY_MATE)
    vmem = pl.BlockSpec(memory_space=pltpu.VMEM)
    smem = pl.BlockSpec(memory_space=pltpu.SMEM)
    return pl.pallas_call(
        functools.partial(gather_kernel, depth),
        out_shape=(
            pltpu.VMEM((2 * depth, FEAT, FEAT), jnp.bfloat16),
            pltpu.VMEM((block_rows, FEAT), jnp.float32),
            pltpu.VMEM((tiles, TILE, TILE), jnp.bfloat16),
        ),
        in_specs=[smem, smem, vmem, vmem, vmem, vmem, pl.BlockSpec(memory_space=pl.ANY)],
        out_specs=(vmem, vmem, vmem),
        scratch_shapes=[
            pltpu.VMEM((FEAT, 2 * FEAT), jnp.bfloat16),
            pltpu.VMEM((4, 2 * FEAT, TILE), jnp.float32),
            pltpu.VMEM(rows.shape, jnp.float32),
            pltpu.VMEM(dense_blocks.shape, jnp.bfloat16),
            pltpu.SemaphoreType.DMA((sems,)),
            pltpu.SemaphoreType.DMA((sems,)),
            pltpu.SemaphoreType.DMA,
        ],
        compiler_params=pltpu.CompilerParams(collective_id=0, has_side_effects=True, vmem_limit_bytes=67043328 - 10 * 2**20 - 65536),
        name="gather_and_prepare",
    )(labels, counts, features, rows, cols, strength, dense_blocks)


def place_kernel(depth, source, dest, got, mats, dense, out, acc):
    acc[...] = jnp.zeros_like(acc)
    me = lax.axis_index("row")
    half = depth // 2
    group = 8

    def spot(i):
        listed = source[0, i]
        block = lax.div(listed, 2)
        offset = lax.rem(lax.div(block, 2) - lax.div(me, 2) + half - 1 + depth, depth)
        return (offset * 2 + lax.rem(block + me, 2)) * 2 + lax.rem(listed, 2)

    def body(g, carry):
        terms = [
            jnp.dot(
                mats[g * group + k], got[spot(g * group + k)], preferred_element_type=jnp.float32
            )
            for k in range(group)
        ]
        for k in range(group):
            rows = pl.ds(pl.multiple_of(dest[0, g * group + k] * TILE, TILE), TILE)
            acc[rows, :] += terms[k]
        return carry

    lax.fori_loop(0, mats.shape[0] // group, body, 0)
    out[...] = (acc[...] + dense[...]).astype(jnp.bfloat16)


def place_tiles(source, dest, got, mats, acc):
    vmem = pl.BlockSpec(memory_space=pltpu.VMEM)
    smem = pl.BlockSpec(memory_space=pltpu.SMEM)
    return pl.pallas_call(
        functools.partial(place_kernel, lax.axis_size("row") // 2),
        out_shape=jax.ShapeDtypeStruct(acc.shape, jnp.bfloat16),
        in_specs=[smem, smem, vmem, vmem, vmem],
        out_specs=vmem,
        scratch_shapes=[pltpu.VMEM(acc.shape, jnp.float32)],
        compiler_params=pltpu.CompilerParams(vmem_limit_bytes=20 * 2**20),
        name="place_tiles",
    )(source, dest, got, mats, acc)


def scatter_kernel(
    part, weight, bias, out, from_core, sum_core, from_one, sum_one, from_two, sum_two, from_x, send_sem, recv_sem
):
    me = lax.axis_index("rep")
    core = me % 2
    y = (me // 2) % 4
    x = me // 8

    def rep_of(xx, yy, cc):
        return (xx * 4 + yy) * 2 + cc

    flips = (y, y + 1 - 2 * (y % 2), (y + 2) % 4, 3 - y)
    mate = {"rep": rep_of(x, y, 1 - core)}
    y_peer = {1: {"rep": rep_of(x, flips[1], core)}, 3: {"rep": rep_of(x, flips[3], core)}}
    x_peer = {"rep": rep_of(1 - x, y, core)}
    barrier = pltpu.get_barrier_semaphore()
    for peer in (mate, y_peer[1], y_peer[3], x_peer):
        pl.semaphore_signal(barrier, inc=1, device_id=peer, device_id_type=MESH)
    pl.semaphore_wait(barrier, 4)

    def piece(h, q, t, cc):
        xx = x if q == 0 else 1 - x
        first = rep_of(xx, flips[t], cc) * (2 * TILE) + h * TILE
        return part.at[pl.ds(pl.multiple_of(first, TILE), TILE)]

    def number(h, q, t):
        return (h * 2 + q) * 4 + t

    def remote(source, target, index, peer):
        return pltpu.make_async_remote_copy(
            src_ref=source,
            dst_ref=target,
            send_sem=send_sem.at[index],
            recv_sem=recv_sem.at[index],
            device_id=peer,
            device_id_type=MESH,
        )

    def core_copy(h, q, t):
        n = number(h, q, t)
        return remote(piece(h, q, t, 1 - core), from_core.at[n], n, mate)

    def one_copy(h, q, t):
        way = HALVES[h][0]
        arrives = {1: {1: 0, 2: 3}, 3: {3: 0, 2: 1}}[way][t]
        slot = (h * 2 + q) * 2 + (0 if arrives == 0 else 1)
        return remote(sum_core.at[slot], from_one.at[slot], 16 + slot, y_peer[way])

    def two_copy(h, q):
        slot = h * 2 + q
        return remote(sum_two.at[slot], from_two.at[slot], 24 + slot, y_peer[HALVES[h][1]])

    def x_copy(h):
        return remote(sum_one.at[h], from_x.at[h], 28 + h, x_peer)

    def wide(ref):
        return ref[...].astype(jnp.float32)

    started = []

    def begin(copy):
        copy.start()
        started.append(copy)

    def send_one(h, q, t):
        copy = one_copy(h, q, t)
        core_copy(h, q, t).wait_recv()
        slot = (h * 2 + q) * 2 + (0 if t == HALVES[h][0] else 1)
        sum_core[slot] = (
            wide(piece(h, q, t, core)) + wide(from_core.at[number(h, q, t)])
        ).astype(jnp.bfloat16)
        begin(copy)

    def send_two(h, q, t):
        core_copy(h, q, t).wait_recv()
        one_copy(h, q, 2).wait_recv()
        sum_two[h * 2 + q] = (
            wide(piece(h, q, t, core))
            + wide(from_core.at[number(h, q, t)])
            + wide(from_one.at[(h * 2 + q) * 2 + 1])
        ).astype(jnp.bfloat16)
        begin(two_copy(h, q))

    plan = []
    for send, q, place in (
        (send_one, 1, None),
        (send_one, 1, 0),
        (send_one, 0, None),
        (send_two, 1, 1),
        (send_one, 0, 0),
        (send_two, 0, 1),
    ):
        for h in (0, 1):
            plan.append((send, (h, q, 2 if place is None else HALVES[h][place])))
    for send, key in plan:
        begin(core_copy(*key))
    for q in (1, 0):
        for h in (0, 1):
            begin(core_copy(h, q, 0))
    for send, key in plan:
        send(*key)

    def total(h, q):
        core_copy(h, q, 0).wait_recv()
        one_copy(h, q, HALVES[h][0]).wait_recv()
        two_copy(h, q).wait_recv()
        return (
            wide(piece(h, q, 0, core))
            + wide(from_core.at[number(h, q, 0)])
            + wide(from_one.at[(h * 2 + q) * 2])
            + wide(from_two.at[h * 2 + q])
        )

    for h in (0, 1):
        sum_one[h] = total(h, 1).astype(jnp.bfloat16)
        begin(x_copy(h))
    for h in (0, 1):
        own = total(h, 0)
        x_copy(h).wait_recv()
        hidden = (own + wide(from_x.at[h])).astype(jnp.bfloat16)
        projected = jnp.dot(hidden, weight[...], preferred_element_type=jnp.float32) + bias[...]
        out[pl.ds(h * TILE, TILE), :] = jnp.maximum(projected, 0.0).astype(jnp.bfloat16)
    for copy in started:
        copy.wait_send()


def scatter_and_project(part, weight, bias):
    vmem = pl.BlockSpec(memory_space=pltpu.VMEM)

    def tiles(n):
        return pltpu.VMEM((n, TILE, FEAT), jnp.bfloat16)

    return pl.pallas_call(
        scatter_kernel,
        out_shape=jax.ShapeDtypeStruct((2 * TILE, FEAT), jnp.bfloat16),
        in_specs=[vmem, vmem, vmem],
        out_specs=vmem,
        scratch_shapes=[
            tiles(16),
            tiles(8),
            tiles(8),
            tiles(2),
            tiles(4),
            tiles(4),
            tiles(2),
            pltpu.SemaphoreType.DMA((30,)),
            pltpu.SemaphoreType.DMA((30,)),
        ],
        compiler_params=pltpu.CompilerParams(collective_id=1, has_side_effects=True, vmem_limit_bytes=10 * 2**20),
        name="scatter_and_project",
    )(part, weight, bias)


def shards(
    features,
    dense_blocks,
    thick_neighbour_labels,
    tile_source,
    tile_dest,
    entry_rows,
    entry_cols,
    edge_strength_list,
    entry_count,
    weight,
    out_bias,
):
    depth = lax.axis_size("row") // 2
    got, acc, mats = gather_and_prepare(
        features,
        dense_blocks,
        thick_neighbour_labels,
        entry_count[0],
        entry_rows[0, 0],
        entry_cols[0, 0],
        edge_strength_list[0, 0],
    )
    part = place_tiles(
        tile_source[0],
        tile_dest[0],
        got.reshape(4 * depth, TILE, FEAT),
        mats,
        acc,
    )
    return scatter_and_project(part, weight, out_bias.reshape(1, FEAT))


def solution(mesh):
    return jax.shard_map(
        shards,
        mesh=mesh,
        in_specs=(
            P(("row", "rep"), None),
            P("row", None, "rep"),
            P("row", None),
            P("row", "rep", None),
            P("row", "rep", None),
            P("row", "rep", None, None),
            P("row", "rep", None, None),
            P("row", "rep", None, None),
            P("row", "rep", None),
            P(),
            P(),
        ),
        out_specs=P(("row", "rep"), None),
        check_vma=False,
    )
```
